32 devices in a mesh: grp: 8 (over z, x), hd: 4 (over y, core).
Axes of the slice: x: 2, y: 2, z: 4, core: 2. Of those that a mesh axis runs over, the one named last changes fastest.
Arguments:
- query_states: bfloat16 [4096, 2048], P(('grp', 'hd')), may hold values from -8 to 8
- key_states: bfloat16 [4096, 2048], P(('grp', 'hd')), may hold values from -8 to 8
- value_states: bfloat16 [4096, 2048], P(('grp', 'hd')), may hold values from -6 to 6
- output_cotangent: bfloat16 [4096, 2048], P(('grp', 'hd')), may hold values from -6 to 6
- pattern: int32 [32, 2], replicated, may hold values from 0 to 31, as said below
Outputs:
- attended: bfloat16 [4096, 2048], P(('grp', 'hd'))
- query_gradient: bfloat16 [4096, 2048], P(('grp', 'hd'))
- key_gradient: bfloat16 [4096, 2048], P(('grp', 'hd'))
- value_gradient: bfloat16 [4096, 2048], P(('grp', 'hd'))
The draws below stay inside these ranges and needn't reach their ends.
Inputs may be any that keep to these rules, and one draw needn't show every extreme that they name: `pattern`: random columns never name a block of the query's own group. The random columns of one query group name exactly 4 distinct blocks. Counting the window blocks next to the group and the random blocks together, a query group names at most 2 distinct blocks of any one other group, and exactly 2 of some group.
All inputs are finite; a program needn't handle non-finite values.
Results may differ from the reference program's by a relative error of at most 0.01.
Values may be sent and summed in bfloat16 or wider, within the bound.
A program may use at most 128 MiB of HBM per device.

```python
import math
import jax
import jax.numpy as jnp
from jax import lax

HEADS = 16
HEAD_DIM = 128
BLOCK = 128
GLOBALS = 1
RANDOM = 2
GROUPS = 8
GROUP_BLOCKS = 4
BLOCKS = 32
SEQUENCE = 4096
POOL = 4
CAPACITY = 2
KEYS = 6


def paired_states(base_key):
    first_key = jax.random.fold_in(base_key, 41)
    second_key = jax.random.fold_in(base_key, 42)
    scale_key = jax.random.fold_in(base_key, 43)
    columns_all = HEADS * HEAD_DIM
    query_values = jax.random.truncated_normal(first_key, -3.0, 3.0, (SEQUENCE, columns_all), jnp.float32)
    key_values = jax.random.truncated_normal(second_key, -3.0, 3.0, (SEQUENCE, columns_all), jnp.float32)
    row_scale = jnp.exp(jax.random.uniform(scale_key, (SEQUENCE, 1), jnp.float32, math.log(0.4), math.log(2.5)))
    key_values = key_values * row_scale
    return (query_values, key_values)


def draw_query_states(key, part):
    return paired_states(key)[0].astype(jnp.bfloat16)


def draw_key_states(key, part):
    return paired_states(key)[1].astype(jnp.bfloat16)


def pattern_for_group(group_key, group_index):
    groups_range = jnp.arange(GROUPS, dtype=jnp.int32)
    beside = (groups_range == group_index - 1) | (groups_range == group_index + 1)
    barred = beside | (groups_range == group_index)
    order_key = jax.random.fold_in(group_key, 1)
    ticket_key = jax.random.fold_in(group_key, 2)
    local_key = jax.random.fold_in(group_key, 3)
    entry_key = jax.random.fold_in(group_key, 4)
    group_scores = jax.random.permutation(order_key, GROUPS).astype(jnp.int32) + jnp.where(barred, 4 * GROUPS, 0)
    full_group = jnp.argmin(group_scores).astype(jnp.int32)
    ticket_ids = jnp.arange(GROUPS * CAPACITY, dtype=jnp.int32)
    ticket_group = ticket_ids // CAPACITY
    ticket_copy = ticket_ids % CAPACITY
    copy_limit = CAPACITY - beside[ticket_group].astype(jnp.int32)
    usable = (ticket_group != group_index) & (ticket_copy < copy_limit)
    priority = jax.random.permutation(ticket_key, GROUPS * CAPACITY).astype(jnp.int32)
    priority = jnp.where(ticket_group == full_group, priority - GROUPS * CAPACITY, priority)
    priority = jnp.where(usable, priority, priority + 4 * GROUPS * CAPACITY)
    chosen = jnp.argsort(priority)[:POOL]
    chosen_group = ticket_group[chosen]
    pool_order = jnp.arange(POOL)
    earlier = (chosen_group[:, None] == chosen_group[None, :]) & (pool_order[None, :] < pool_order[:, None])
    chosen_rank = jnp.sum(earlier.astype(jnp.int32), axis=1)
    local_orders = jax.vmap(lambda sub_key: jax.random.permutation(sub_key, GROUP_BLOCKS))(jax.random.split(local_key, GROUPS)).astype(jnp.int32)
    pooled = chosen_group * GROUP_BLOCKS + local_orders[chosen_group, chosen_rank]
    readers = jax.random.permutation(entry_key, GROUP_BLOCKS * RANDOM).astype(jnp.int32) % POOL
    return pooled[readers].reshape(GROUP_BLOCKS, RANDOM)


def draw_pattern(key, part):
    group_keys = jax.random.split(jax.random.fold_in(key, 7), GROUPS)
    return jax.vmap(pattern_for_group)(group_keys, jnp.arange(GROUPS, dtype=jnp.int32)).reshape(BLOCKS, RANDOM).astype(jnp.int32)


def shard_levels(rng, shape, pieces, low, largest):
    factor_of, own = 1.0, jax.random.fold_in(rng, 6)
    for axis_at, blocks in pieces:
        heights = jnp.exp(jax.random.uniform(jax.random.fold_in(own, axis_at), (blocks,), jnp.float32, low / len(pieces), largest / len(pieces)))
        factor_of = factor_of * jnp.repeat(heights, shape[axis_at] // blocks).reshape([-1 if axis == axis_at else 1 for axis in range(len(shape))])
    return factor_of


def normal_values(stream_key, extent, spread, bound, shards=(), held_as=jnp.bfloat16):
    entries = jax.random.normal(stream_key, extent, jnp.float32) * spread
    if len(shards) > 0:
        entries = shard_levels(stream_key, extent, shards, -0.22, 0.18) * entries
    return jnp.clip(entries, min=-bound, max=bound).astype(held_as)


def setup_inputs(seed: int = 0) -> dict:
    seeds = jax.random.split(jax.random.key(seed), 6)
    query_states = draw_query_states(jax.random.fold_in(seeds[5], 71), 0)
    key_states = draw_key_states(jax.random.fold_in(seeds[5], 71), 0)
    value_states = normal_values(seeds[2], (SEQUENCE, HEADS * HEAD_DIM), 1.0, 6.0, ((0, 32),))
    output_cotangent = normal_values(seeds[3], (SEQUENCE, HEADS * HEAD_DIM), 1.0, 6.0, ((0, 32),))
    pattern = draw_pattern(jax.random.fold_in(seeds[5], 71), 0)
    return {"query_states": query_states, "key_states": key_states, "value_states": value_states, "output_cotangent": output_cotangent, "pattern": pattern}


mask_value = -1e+30

def reference(query_states, key_states, value_states, output_cotangent, pattern):
    score_scale = 1.0 / math.sqrt(HEAD_DIM)
    shape_blocks = (BLOCKS, BLOCK, HEADS, HEAD_DIM)
    query_blocks = query_states.reshape(shape_blocks)
    key_blocks = key_states.reshape(shape_blocks)
    value_blocks = value_states.reshape(shape_blocks)
    cotangent_blocks = output_cotangent.reshape(shape_blocks)
    block_ids = jnp.arange(BLOCKS, dtype=jnp.int32)
    global_ids = jnp.broadcast_to(jnp.arange(GLOBALS, dtype=jnp.int32)[None, :], (BLOCKS, GLOBALS))
    raw_lists = jnp.concatenate([(block_ids - 1)[:, None], block_ids[:, None], (block_ids + 1)[:, None], global_ids, pattern.astype(jnp.int32)], axis=1)
    valid_lists = (raw_lists >= 0) & (raw_lists < BLOCKS)
    key_lists = jnp.clip(raw_lists, 0, BLOCKS - 1).astype(jnp.int32)
    columns = jnp.arange(KEYS)
    rows_here = jnp.arange(GROUP_BLOCKS)
    edge_entries = (rows_here[:, None] == 0) & (columns[None, :] == 0) | (rows_here[:, None] == GROUP_BLOCKS - 1) & (columns[None, :] == 2)
    direct = ((columns[None, :] < 3 + GLOBALS) & jnp.logical_not(edge_entries))[:, :, None, None, None]
    entry_count = GROUP_BLOCKS * RANDOM + 2
    order_ids = jnp.arange(entry_count)
    feature_count = BLOCK * HEADS * HEAD_DIM

    def remote_terms(lists_here, terms):
        entry_ids = jnp.concatenate([lists_here[:, 3 + GLOBALS:].reshape(-1), lists_here[0, 0:1], lists_here[GROUP_BLOCKS - 1, 2:3]]).astype(jnp.int32)
        flat_terms = jnp.concatenate([terms[:, 3 + GLOBALS:].reshape(-1, feature_count), terms[0, 0].reshape(1, -1), terms[GROUP_BLOCKS - 1, 2].reshape(1, -1)], axis=0)
        same_block = entry_ids[:, None] == entry_ids[None, :]
        repeated = jnp.any(same_block & (order_ids[None, :] < order_ids[:, None]), axis=1)
        summed = jnp.dot(same_block.astype(jnp.float32), flat_terms, precision=lax.Precision.HIGHEST)
        rounded = lax.optimization_barrier(summed.astype(jnp.bfloat16)).astype(jnp.float32)
        return (entry_ids, jnp.where(repeated[:, None], 0.0, rounded).reshape(entry_count, BLOCK, HEADS, HEAD_DIM))

    def group_step(accumulators, group_index):
        key_total, value_total = accumulators
        first_block = group_index * GROUP_BLOCKS
        lists_here = lax.dynamic_slice_in_dim(key_lists, first_block, GROUP_BLOCKS, 0)
        valid_here = lax.dynamic_slice_in_dim(valid_lists, first_block, GROUP_BLOCKS, 0)
        queries_here = lax.dynamic_slice_in_dim(query_blocks, first_block, GROUP_BLOCKS, 0).astype(jnp.float32)
        cotangent_here = lax.dynamic_slice_in_dim(cotangent_blocks, first_block, GROUP_BLOCKS, 0).astype(jnp.float32)
        keys_here = key_blocks[lists_here].astype(jnp.float32)
        values_here = value_blocks[lists_here].astype(jnp.float32).reshape(GROUP_BLOCKS, KEYS * BLOCK, HEADS, HEAD_DIM)
        scores = jnp.einsum('qthd,qkshd->qhtks', queries_here, keys_here) * score_scale
        scores = jnp.where(valid_here[:, None, None, :, None], scores, mask_value).reshape(GROUP_BLOCKS, HEADS, BLOCK, KEYS * BLOCK)
        row_peaks = lax.optimization_barrier(jnp.max(scores, axis=-1, keepdims=True))
        weights = jnp.exp(scores - row_peaks)
        totals = lax.optimization_barrier(jnp.sum(weights, axis=-1, keepdims=True))
        soft_weights = lax.optimization_barrier((weights / totals).astype(jnp.bfloat16)).astype(jnp.float32)
        attended = jnp.einsum('qhtn,qnhd->qthd', soft_weights, values_here).astype(jnp.bfloat16)
        row_delta = lax.optimization_barrier(jnp.sum(cotangent_here * attended.astype(jnp.float32), axis=-1))
        row_delta = jnp.transpose(row_delta, (0, 2, 1))[..., None]
        prob_grad = jnp.einsum('qthd,qnhd->qhtn', cotangent_here, values_here)
        score_grad = lax.optimization_barrier((soft_weights * (prob_grad - row_delta) * score_scale).astype(jnp.bfloat16)).astype(jnp.float32)
        key_flat = keys_here.reshape(GROUP_BLOCKS, KEYS * BLOCK, HEADS, HEAD_DIM)
        query_grad = jnp.einsum('qhtn,qnhd->qthd', score_grad, key_flat).astype(jnp.bfloat16)
        key_terms = jnp.einsum('qhtn,qthd->qnhd', score_grad, queries_here).reshape(GROUP_BLOCKS, KEYS, BLOCK, HEADS, HEAD_DIM)
        value_terms = jnp.einsum('qhtn,qthd->qnhd', soft_weights, cotangent_here).reshape(GROUP_BLOCKS, KEYS, BLOCK, HEADS, HEAD_DIM)
        key_total = key_total.at[lists_here].add(jnp.where(direct, key_terms, 0.0))
        value_total = value_total.at[lists_here].add(jnp.where(direct, value_terms, 0.0))
        entry_ids, key_remote = remote_terms(lists_here, key_terms)
        entry_ids, value_remote = remote_terms(lists_here, value_terms)
        key_total = key_total.at[entry_ids].add(key_remote)
        value_total = value_total.at[entry_ids].add(value_remote)
        return ((key_total, value_total), (attended, query_grad))
    zero_total = jnp.zeros(shape_blocks, jnp.float32)
    totals_out, group_out = lax.scan(group_step, (zero_total, zero_total), jnp.arange(GROUPS, dtype=jnp.int32))
    flat_shape = (SEQUENCE, HEADS * HEAD_DIM)
    return (group_out[0].reshape(flat_shape), group_out[1].reshape(flat_shape), totals_out[0].astype(jnp.bfloat16).reshape(flat_shape), totals_out[1].astype(jnp.bfloat16).reshape(flat_shape))
```

```python
import functools
import math

import jax
import jax.numpy as jnp
from jax import lax
from jax.experimental import pallas as pl
from jax.experimental.pallas import tpu as pltpu
from jax.sharding import PartitionSpec as P

HEADS = 16
HEAD_DIM = 128
BLOCK = 128
GLOBALS = 1
RANDOM = 2
MASK_VALUE = -1e30
VMEM_BYTES = 60 * 1024 * 1024
MESH = pl.DeviceIdType.MESH


def place(team, hd_size):
    index = lax.axis_index("grp") * hd_size + lax.axis_index("hd")
    return index // team, index % team


def target(number, hd_size):
    return (number // hd_size, number % hd_size)


def far_first(step):
    return 1 + (HEADS // 2 - 1 + step) % (HEADS - 1)


def enter(head, member, team, hd_size):
    barrier = pltpu.get_barrier_semaphore()

    def greet(number):
        pl.semaphore_signal(barrier, inc=1, device_id=target(number, hd_size), device_id_type=MESH)

    @pl.loop(1, HEADS)
    def _(step):
        greet((head + step) % HEADS * team + member)

    @pl.loop(1, team)
    def _(step):
        greet(head * team + (member + step) % team)

    pl.semaphore_wait(barrier, HEADS - 1 + team - 1)


def columns(head):
    return pl.ds(pl.multiple_of(head * HEAD_DIM, HEAD_DIM), HEAD_DIM)


def gather_kernel(
    team, hd_size, q_in, k_in, v_in, g_in, q_out, k_out, v_out, g_out,
    send_sem, recv_sem, own_sem, pass_send, pass_recv,
):
    head, member = place(team, hd_size)
    enter(head, member, team, hd_size)
    arrays = (
        (k_in, lambda at: k_out.at[at, member]),
        (v_in, lambda at: v_out.at[at, member]),
        (q_in, lambda at: q_out.at[at]),
        (g_in, lambda at: g_out.at[at]),
    )

    def remote(number, peer):
        source, dest = arrays[number]
        return pltpu.make_async_remote_copy(
            source.at[:, columns(peer)], dest(head), send_sem.at[number, peer],
            recv_sem.at[number, head], device_id=target(peer * team + member, hd_size),
            device_id_type=MESH,
        )

    def arrival(number, peer):
        source, dest = arrays[number]
        return pltpu.make_async_remote_copy(
            source.at[:, columns(peer)], dest(peer), send_sem.at[number, peer],
            recv_sem.at[number, peer], device_id=target(peer * team + member, hd_size),
            device_id_type=MESH,
        )

    def own(number):
        source, dest = arrays[number]
        return pltpu.make_async_copy(source.at[:, columns(head)], dest(head), own_sem.at[number])

    def shared(number, block, other, owner):
        ref = (k_out, v_out)[number]
        return pltpu.make_async_remote_copy(
            ref.at[block, owner], ref.at[block, owner], pass_send.at[number, block, other],
            pass_recv.at[number, block, owner], device_id=target(head * team + other, hd_size),
            device_id_type=MESH,
        )

    def share(number, block):
        @pl.loop(1, team)
        def _(step):
            shared(number, block, (member + step) % team, member).start()

    for number in range(4):
        own(number).start()

    for pair in ((0, 1), (2, 3)):
        @pl.loop(0, HEADS - 1)
        def _(step):
            peer = (head + far_first(step)) % HEADS
            for number in pair:
                remote(number, peer).start()

    for number in range(4):
        own(number).wait()
    for number in range(2):
        share(number, head)

    @pl.loop(0, HEADS - 1)
    def _(step):
        peer = (head + HEADS - far_first(step)) % HEADS
        for number in range(2):
            arrival(number, peer).wait_recv()
            share(number, peer)

    @pl.loop(0, HEADS - 1)
    def _(step):
        peer = (head + HEADS - far_first(step)) % HEADS
        for number in (2, 3):
            arrival(number, peer).wait_recv()

    @pl.loop(0, HEADS - 1)
    def _(step):
        peer = (head + far_first(step)) % HEADS
        for number in range(4):
            remote(number, peer).wait_send()

    @pl.loop(1, team)
    def _(step):
        other = (member + step) % team

        @pl.loop(0, HEADS)
        def _(block):
            for number in range(2):
                shared(number, block, other, member).wait_send()
                shared(number, block, other, other).wait_recv()


def dot(a, b, a_dim, b_dim):
    return lax.dot_general(
        a, b, (((a_dim,), (b_dim,)), ((), ())), preferred_element_type=jnp.float32
    )


def attention_kernel(team, hd_size, pattern, q_ref, g_ref, k_ref, v_ref, o_ref, dq_ref, dk_ref, dv_ref):
    _, member = place(team, hd_size)
    blocks = k_ref.shape[0]
    scale = 1.0 / math.sqrt(HEAD_DIM)

    @pl.loop(0, blocks)
    def _(at):
        dk_ref[at] = jnp.zeros((BLOCK, HEAD_DIM), jnp.float32)
        dv_ref[at] = jnp.zeros((BLOCK, HEAD_DIM), jnp.float32)

    def step(at):
        block = at * team + member
        left_ok, right_ok = block >= 1, block + 1 < blocks
        ids = [jnp.maximum(block - 1, 0), block, jnp.minimum(block + 1, blocks - 1)]
        ids += list(range(GLOBALS)) + [pattern[block, r] for r in range(RANDOM)]
        allowed = [left_ok, None, right_ok] + [None] * (GLOBALS + RANDOM)
        queries, cotangent = q_ref[at], g_ref[at]
        keys = jnp.concatenate([k_ref[i] for i in ids], axis=0)
        values = jnp.concatenate([v_ref[i] for i in ids], axis=0)
        scores = dot(keys, queries, 1, 1) * scale
        parts = []
        for entry, ok in enumerate(allowed):
            part = scores[entry * BLOCK : (entry + 1) * BLOCK]
            parts.append(part if ok is None else jnp.where(ok, part, MASK_VALUE))
        scores = jnp.concatenate(parts, axis=0)
        weights = jnp.exp(scores - jnp.max(scores, axis=0, keepdims=True))
        total = jnp.sum(weights, axis=0, keepdims=True)
        soft = (weights * (1.0 / total)).astype(jnp.bfloat16)
        prob_grad = dot(values, cotangent, 1, 1)
        wide = soft.astype(jnp.float32)
        delta = jnp.sum(wide * prob_grad, axis=0, keepdims=True)
        score_grad = (wide * ((prob_grad - delta) * scale)).astype(jnp.bfloat16)
        o_ref[at] = dot(soft, values, 0, 0).astype(o_ref.dtype)
        dq_ref[at] = dot(score_grad, keys, 0, 0).astype(dq_ref.dtype)
        key_terms = dot(score_grad, queries, 1, 0)
        value_terms = dot(soft, cotangent, 1, 0)
        for entry, i in enumerate(ids):
            rows = slice(entry * BLOCK, (entry + 1) * BLOCK)
            dk_ref[i] += key_terms[rows]
            dv_ref[i] += value_terms[rows]

    @pl.loop(0, HEADS)
    def _(at):
        step(at)


def scatter_kernel(
    team, hd_size, o_in, dq_in, dk_in, dv_in, o_out, dq_out, dk_out, dv_out,
    mine, theirs, summed, send_sem, recv_sem, own_sem, pass_send, pass_recv, load_sem,
):
    head, member = place(team, hd_size)
    parts = (dk_in, dv_in)
    arrays = (
        (lambda at: o_in.at[at], o_out),
        (lambda at: dq_in.at[at], dq_out),
        (lambda at: summed.at[0, at], dk_out),
        (lambda at: summed.at[1, at], dv_out),
    )

    def load(number):
        return pltpu.make_async_copy(
            parts[number].at[:, member], mine.at[number], load_sem.at[number]
        )

    for number in range(2):
        load(number).start()
    enter(head, member, team, hd_size)

    def shared(number, block, step, other):
        return pltpu.make_async_remote_copy(
            parts[number].at[block, other], theirs.at[step - 1, number, block],
            pass_send.at[step - 1, number, block], pass_recv.at[step - 1, number, block],
            device_id=target(head * team + other, hd_size), device_id_type=MESH,
        )

    def remote(number, peer):
        source, dest = arrays[number]
        return pltpu.make_async_remote_copy(
            source(peer), dest.at[:, columns(head)], send_sem.at[number, peer],
            recv_sem.at[number, head], device_id=target(peer * team + member, hd_size),
            device_id_type=MESH,
        )

    def arrival(number, peer):
        source, dest = arrays[number]
        return pltpu.make_async_remote_copy(
            source(peer), dest.at[:, columns(peer)], send_sem.at[number, peer],
            recv_sem.at[number, peer], device_id=target(peer * team + member, hd_size),
            device_id_type=MESH,
        )

    def own(number):
        source, dest = arrays[number]
        return pltpu.make_async_copy(source(head), dest.at[:, columns(head)], own_sem.at[number])

    @pl.loop(0, HEADS)
    def _(turn):
        block = (head + far_first(turn % (HEADS - 1)) * (1 - turn // (HEADS - 1))) % HEADS

        @pl.loop(1, team)
        def _(step):
            for number in range(2):
                shared(number, block, step, (member + step) % team).start()

    @pl.loop(0, HEADS - 1)
    def _(step):
        peer = (head + far_first(step)) % HEADS
        for number in range(2):
            remote(number, peer).start()

    for number in range(2):
        own(number).start()
    for number in range(2):
        load(number).wait()

    def add(block):
        @pl.loop(1, team)
        def _(step):
            for number in range(2):
                shared(number, block, step, (member + step) % team).wait_recv()
        for number in range(2):
            summed[number, block] = lax.fori_loop(
                0, team - 1, lambda step, total: total + theirs[step, number, block],
                mine[number, block],
            ).astype(summed.dtype)

    add((head + far_first(0)) % HEADS)

    @pl.loop(0, HEADS - 1)
    def _(step):
        later = step + 1
        add((head + far_first(later % (HEADS - 1)) * (1 - later // (HEADS - 1))) % HEADS)
        peer = (head + far_first(step)) % HEADS
        for number in (2, 3):
            remote(number, peer).start()

    for number in (2, 3):
        own(number).start()

    @pl.loop(0, HEADS - 1)
    def _(step):
        peer = (head + HEADS - far_first(step)) % HEADS
        for number in range(4):
            arrival(number, peer).wait_recv()

    @pl.loop(0, HEADS - 1)
    def _(step):
        peer = (head + far_first(step)) % HEADS
        for number in range(4):
            remote(number, peer).wait_send()

    @pl.loop(1, team)
    def _(step):
        @pl.loop(0, HEADS)
        def _(block):
            for number in range(2):
                shared(number, block, step, (member + step) % team).wait_send()

    for number in range(4):
        own(number).wait()


def on_device(query_states, key_states, value_states, output_cotangent, pattern):
    hd_size = lax.axis_size("hd")
    devices = lax.axis_size("grp") * hd_size
    team = devices // HEADS
    blocks = pattern.shape[0]
    bf16, f32 = jnp.bfloat16, jnp.float32
    dma = pltpu.SemaphoreType.DMA
    anywhere = pl.BlockSpec(memory_space=pl.ANY)
    vmem = pl.BlockSpec(memory_space=pltpu.VMEM)
    tile = (BLOCK, HEAD_DIM)
    own_shape = jax.ShapeDtypeStruct((HEADS, *tile), bf16)
    all_shape = jax.ShapeDtypeStruct((HEADS, team, *tile), bf16)
    part_shape = jax.ShapeDtypeStruct((blocks, *tile), f32)

    queries, keys, values, cotangent = pl.pallas_call(
        functools.partial(gather_kernel, team, hd_size),
        out_shape=(own_shape, all_shape, all_shape, own_shape),
        in_specs=[anywhere] * 4,
        out_specs=(anywhere,) * 4,
        scratch_shapes=[
            dma((4, HEADS)), dma((4, HEADS)), dma((4,)),
            dma((2, HEADS, team)), dma((2, HEADS, team)),
        ],
        compiler_params=pltpu.CompilerParams(collective_id=0, has_side_effects=True),
        name="gather_heads",
    )(query_states, key_states, value_states, output_cotangent)

    attended, query_grad, key_part, value_part = pl.pallas_call(
        functools.partial(attention_kernel, team, hd_size),
        out_shape=(own_shape, own_shape, part_shape, part_shape),
        in_specs=[pl.BlockSpec(memory_space=pltpu.SMEM)] + [vmem] * 4,
        out_specs=(vmem,) * 4,
        compiler_params=pltpu.CompilerParams(vmem_limit_bytes=VMEM_BYTES),
        name="attention",
    )(pattern, queries, cotangent, keys.reshape(blocks, *tile), values.reshape(blocks, *tile))

    out_shape = jax.ShapeDtypeStruct(query_states.shape, bf16)
    return pl.pallas_call(
        functools.partial(scatter_kernel, team, hd_size),
        out_shape=(out_shape,) * 4,
        in_specs=[anywhere] * 4,
        out_specs=(anywhere,) * 4,
        scratch_shapes=[
            pltpu.VMEM((2, HEADS, *tile), f32),
            pltpu.VMEM((team - 1, 2, HEADS, *tile), f32),
            pltpu.VMEM((2, HEADS, *tile), bf16),
            dma((4, HEADS)), dma((4, HEADS)), dma((4,)),
            dma((team - 1, 2, HEADS)), dma((team - 1, 2, HEADS)), dma((2,)),
        ],
        compiler_params=pltpu.CompilerParams(
            collective_id=1, has_side_effects=True, vmem_limit_bytes=VMEM_BYTES
        ),
        name="scatter_heads",
    )(
        attended, query_grad,
        key_part.reshape(HEADS, team, *tile), value_part.reshape(HEADS, team, *tile),
    )


def solution(mesh):
    split = P(("grp", "hd"), None)
    return jax.shard_map(
        on_device, mesh=mesh, in_specs=(split,) * 4 + (P(),), out_specs=(split,) * 4,
        check_vma=False,
    )
```

```python
import functools
import math

import jax
import jax.numpy as jnp
from jax import lax
from jax.experimental import pallas as pl
from jax.experimental.pallas import tpu as pltpu
from jax.sharding import PartitionSpec as P

HEADS = 16
HEAD_DIM = 128
BLOCK = 128
GLOBALS = 1
RANDOM = 2
MASK_VALUE = -1e30
VMEM_BYTES = 60 * 1024 * 1024
MESH = pl.DeviceIdType.MESH


def place(team, hd_size):
    index = lax.axis_index("grp") * hd_size + lax.axis_index("hd")
    return index // team, index % team


def target(number, hd_size):
    return (number // hd_size, number % hd_size)


def offset(turn):
    return (1 + (HEADS // 2 - 2 + turn) % (HEADS - 1)) * ((turn + HEADS - 1) // HEADS)


def enter(head, member, team, hd_size):
    barrier = pltpu.get_barrier_semaphore()

    def greet(number):
        pl.semaphore_signal(barrier, inc=1, device_id=target(number, hd_size), device_id_type=MESH)

    @pl.loop(1, HEADS)
    def _(step):
        greet((head + step) % HEADS * team + member)

    @pl.loop(1, team)
    def _(step):
        greet(head * team + (member + step) % team)

    pl.semaphore_wait(barrier, HEADS - 1 + team - 1)


def columns(head):
    return pl.ds(pl.multiple_of(head * HEAD_DIM, HEAD_DIM), HEAD_DIM)


def dot(a, b, a_dim, b_dim):
    return lax.dot_general(
        a, b, (((a_dim,), (b_dim,)), ((), ())), preferred_element_type=jnp.float32
    )


def kernel(
    team, hd_size, pattern, q_in, k_in, v_in, g_in, o_out, dq_out, dk_out, dv_out,
    q_buf, g_buf, k_buf, v_buf, o_buf, dq_buf, window, chain, shared_sum, stage, theirs, summed,
    previous, latest, in_send, in_recv, in_own, pass_send, pass_recv,
    out_send, out_recv, out_own, team_send, team_recv,
):
    head, member = place(team, hd_size)
    blocks = k_buf.shape[0]
    scale = 1.0 / math.sqrt(HEAD_DIM)
    ins = (
        (k_in, lambda at: k_buf.at[at * team + member]),
        (v_in, lambda at: v_buf.at[at * team + member]),
        (q_in, lambda at: q_buf.at[at]),
        (g_in, lambda at: g_buf.at[at]),
    )
    outs = (
        (lambda at: o_buf.at[at], o_out),
        (lambda at: dq_buf.at[at], dq_out),
        (lambda at: summed.at[0, at], dk_out),
        (lambda at: summed.at[1, at], dv_out),
    )

    def receiver(turn):
        return (head + offset(turn)) % HEADS

    def sender(turn):
        return (head + HEADS - offset(turn)) % HEADS

    def in_copy(number, peer, lands):
        source, dest = ins[number]
        return pltpu.make_async_remote_copy(
            source.at[:, columns(peer)], dest(lands), in_send.at[number, peer],
            in_recv.at[number, lands], device_id=target(peer * team + member, hd_size),
            device_id_type=MESH,
        )

    def in_local(number):
        source, dest = ins[number]
        return pltpu.make_async_copy(source.at[:, columns(head)], dest(head), in_own.at[number])

    def pass_copy(number, at, other, owner):
        ref = (k_buf, v_buf)[number].at[at * team + owner]
        return pltpu.make_async_remote_copy(
            ref, ref, pass_send.at[number, at, other], pass_recv.at[number, at, owner],
            device_id=target(head * team + other, hd_size), device_id_type=MESH,
        )

    def out_copy(number, peer, lands):
        source, dest = outs[number]
        return pltpu.make_async_remote_copy(
            source(peer), dest.at[:, columns(lands)], out_send.at[number, peer],
            out_recv.at[number, lands], device_id=target(peer * team + member, hd_size),
            device_id_type=MESH,
        )

    def out_local(number):
        source, dest = outs[number]
        return pltpu.make_async_copy(source(head), dest.at[:, columns(head)], out_own.at[number])

    def team_copy(number, at, step):
        return pltpu.make_async_remote_copy(
            stage.at[step - 1, number, at], theirs.at[step - 1, number, at],
            team_send.at[step - 1, number, at], team_recv.at[step - 1, number, at],
            device_id=target(head * team + (member + step) % team, hd_size), device_id_type=MESH,
        )

    def share(number, at):
        @pl.loop(1, team)
        def _(step):
            pass_copy(number, at, (member + step) % team, member).start()

    for number in range(4):
        in_local(number).start()
    enter(head, member, team, hd_size)

    for pair in ((0, 1), (2, 3)):
        @pl.loop(1, HEADS)
        def _(turn):
            peer = receiver(turn)
            for number in pair:
                in_copy(number, peer, head).start()

    for number in range(4):
        in_local(number).wait()
    for number in range(2):
        share(number, head)

    names = [
        pattern[sender(turn) * team + member, r] for turn in range(HEADS) for r in range(RANDOM)
    ]
    for later in range(len(names)):
        found = jnp.int32(-1)
        for earlier in range(later):
            found = jnp.where(names[earlier] == names[later], earlier, found)
        previous[later] = found

    @pl.loop(0, blocks)
    def _(block):
        found = jnp.int32(-1)
        for entry, name in enumerate(names):
            found = jnp.where(name == block, entry, found)
        latest[block] = found

    zeros = jnp.zeros((BLOCK, HEAD_DIM), jnp.float32)
    for number in range(2):
        shared_sum[number] = zeros
        for role in (0, 2):
            for at in (0, HEADS + 1):
                window[number, role, at] = zeros.astype(window.dtype)

    @pl.loop(1, HEADS)
    def _(turn):
        peer = sender(turn)
        for number in range(2):
            in_copy(number, head, peer).wait_recv()
            share(number, peer)

    @pl.loop(1, team)
    def _(step):
        other = (member + step) % team

        @pl.loop(0, HEADS)
        def _(turn):
            at = sender(turn)
            for number in range(2):
                pass_copy(number, at, other, other).wait_recv()

    def attend(turn, at):
        block = at * team + member
        ids = [jnp.maximum(block - 1, 0), block, jnp.minimum(block + 1, blocks - 1)]
        ids += list(range(GLOBALS)) + [pattern[block, r] for r in range(RANDOM)]
        allowed = [block >= 1, None, block + 1 < blocks] + [None] * (GLOBALS + RANDOM)
        queries, cotangent = q_buf[at], g_buf[at]
        keys = jnp.concatenate([k_buf[i] for i in ids], axis=0)
        values = jnp.concatenate([v_buf[i] for i in ids], axis=0)
        scores = dot(keys, queries, 1, 1) * scale
        parts = []
        for entry, ok in enumerate(allowed):
            part = scores[entry * BLOCK : (entry + 1) * BLOCK]
            parts.append(part if ok is None else jnp.where(ok, part, MASK_VALUE))
        scores = jnp.concatenate(parts, axis=0)
        weights = jnp.exp(scores - jnp.max(scores, axis=0, keepdims=True))
        total = jnp.sum(weights, axis=0, keepdims=True)
        soft = (weights * (1.0 / total)).astype(jnp.bfloat16)
        prob_grad = dot(values, cotangent, 1, 1)
        wide = soft.astype(jnp.float32)
        delta = jnp.sum(wide * prob_grad, axis=0, keepdims=True)
        score_grad = (wide * ((prob_grad - delta) * scale)).astype(jnp.bfloat16)
        o_buf[at] = dot(soft, values, 0, 0).astype(o_buf.dtype)
        dq_buf[at] = dot(score_grad, keys, 0, 0).astype(dq_buf.dtype)
        terms = (dot(score_grad, queries, 1, 0), dot(soft, cotangent, 1, 0))
        for number, term in enumerate(terms):
            entries = [term[e * BLOCK : (e + 1) * BLOCK] for e in range(len(ids))]
            for role in range(3):
                window[number, role, at + 1] = entries[role].astype(window.dtype)
            shared_sum[number] += entries[3]
            for r in range(RANDOM):
                slot = turn * RANDOM + r
                before = previous[slot]
                held = chain[number, jnp.maximum(before, 0)]
                chain[number, slot] = entries[3 + GLOBALS + r] + jnp.where(before >= 0, held, 0.0)

    @pl.loop(0, HEADS)
    def _(turn):
        at = sender(turn)

        @pl.when(turn > 0)
        def _():
            for number in (2, 3):
                in_copy(number, head, at).wait_recv()

        attend(turn, at)

        @pl.when(turn > 1)
        def _():
            before = sender(turn - 1)
            for number in range(2):
                out_copy(number, before, head).start()

    def base(number, block):
        last = latest[block]
        total = jnp.where(last >= 0, chain[number, jnp.maximum(last, 0)], 0.0)
        return total + jnp.where(block == 0, shared_sum[number], 0.0)

    def prepare(at, step):
        block = at * team + (member + step) % team
        for number in range(2):
            total = base(number, block)
            right = window[number, 2, at + 1 - (member + 1) // team].astype(jnp.float32)
            left = window[number, 0, at + 1 + (team - member) // team].astype(jnp.float32)
            total += jnp.where(step == 1, right, 0.0) + jnp.where(step == team - 1, left, 0.0)
            stage[step - 1, number, at] = total.astype(stage.dtype)

    last_peer = sender(HEADS - 1)
    for number in range(2):
        out_copy(number, last_peer, head).start()
        out_local(number).start()

    @pl.loop(1, HEADS + 2)
    def _(turn):
        @pl.when(turn <= HEADS)
        def _():
            @pl.loop(1, team)
            def _(step):
                prepare(receiver(turn % HEADS), step)

        @pl.when(turn > 1)
        def _():
            @pl.loop(1, team)
            def _(step):
                for number in range(2):
                    team_copy(number, receiver((turn - 1) % HEADS), step).start()

    @pl.loop(1, HEADS + 1)
    def _(turn):
        at = receiver(turn % HEADS)

        @pl.loop(1, team)
        def _(step):
            for number in range(2):
                team_copy(number, at, step).wait_recv()

        for number in range(2):
            own = base(number, at * team + member)
            own += window[number, 1, at + 1].astype(jnp.float32)
            summed[number, at] = lax.fori_loop(
                0, team - 1,
                lambda step, total: total + theirs[step, number, at].astype(jnp.float32), own,
            ).astype(summed.dtype)

        @pl.when(turn > 1)
        def _():
            for number in (2, 3):
                out_copy(number, receiver(turn - 1), head).start()

    for number in (2, 3):
        out_local(number).start()

    @pl.loop(1, HEADS)
    def _(turn):
        to, source = receiver(turn), sender(turn)
        for number in range(4):
            in_copy(number, to, head).wait_send()
            out_copy(number, to, head).wait_send()
            out_copy(number, head, source).wait_recv()

    @pl.loop(1, team)
    def _(step):
        @pl.loop(0, HEADS)
        def _(at):
            for number in range(2):
                pass_copy(number, at, (member + step) % team, member).wait_send()
                team_copy(number, at, step).wait_send()

    for number in range(4):
        out_local(number).wait()


def on_device(query_states, key_states, value_states, output_cotangent, pattern):
    hd_size = lax.axis_size("hd")
    devices = lax.axis_size("grp") * hd_size
    team = devices // HEADS
    blocks = pattern.shape[0]
    bf16, f32 = jnp.bfloat16, jnp.float32
    dma = pltpu.SemaphoreType.DMA
    anywhere = pl.BlockSpec(memory_space=pl.ANY)
    tile = (BLOCK, HEAD_DIM)
    out_shape = jax.ShapeDtypeStruct(query_states.shape, bf16)
    return pl.pallas_call(
        functools.partial(kernel, team, hd_size),
        out_shape=(out_shape,) * 4,
        in_specs=[pl.BlockSpec(memory_space=pltpu.SMEM)] + [anywhere] * 4,
        out_specs=(anywhere,) * 4,
        scratch_shapes=[
            pltpu.VMEM((HEADS, *tile), bf16),
            pltpu.VMEM((HEADS, *tile), bf16),
            pltpu.VMEM((blocks, *tile), bf16),
            pltpu.VMEM((blocks, *tile), bf16),
            pltpu.VMEM((HEADS, *tile), bf16),
            pltpu.VMEM((HEADS, *tile), bf16),
            pltpu.VMEM((2, 3, HEADS + 2, *tile), bf16),
            pltpu.VMEM((2, HEADS * RANDOM, *tile), f32),
            pltpu.VMEM((2, *tile), f32),
            pltpu.VMEM((team - 1, 2, HEADS, *tile), bf16),
            pltpu.VMEM((team - 1, 2, HEADS, *tile), bf16),
            pltpu.VMEM((2, HEADS, *tile), bf16),
            pltpu.SMEM((HEADS * RANDOM,), jnp.int32),
            pltpu.SMEM((blocks,), jnp.int32),
            dma((4, HEADS)), dma((4, HEADS)), dma((4,)),
            dma((2, HEADS, team)), dma((2, HEADS, team)),
            dma((4, HEADS)), dma((4, HEADS)), dma((4,)),
            dma((team - 1, 2, HEADS)), dma((team - 1, 2, HEADS)),
        ],
        compiler_params=pltpu.CompilerParams(
            collective_id=0, has_side_effects=True, vmem_limit_bytes=VMEM_BYTES
        ),
        name="head_attention",
    )(pattern, query_states, key_states, value_states, output_cotangent)


def solution(mesh):
    split = P(("grp", "hd"), None)
    return jax.shard_map(
        on_device, mesh=mesh, in_specs=(split,) * 4 + (P(),), out_specs=(split,) * 4,
        check_vma=False,
    )
```

```python
import functools
import math

import jax
import jax.numpy as jnp
from jax import lax
from jax.experimental import pallas as pl
from jax.experimental.pallas import tpu as pltpu
from jax.sharding import PartitionSpec as P

HEADS = 16
HEAD_DIM = 128
BLOCK = 128
GLOBALS = 1
RANDOM = 2
MASK_VALUE = -1e30
VMEM_BYTES = 60 * 1024 * 1024
MESH = pl.DeviceIdType.MESH


def place(team, hd_size):
    index = lax.axis_index("grp") * hd_size + lax.axis_index("hd")
    return index // team, index % team


def target(number, hd_size):
    return (number // hd_size, number % hd_size)


def flip(number, mask, bit):
    a, b = number // bit % 2, mask // bit % 2
    return bit * ((a + b) % 2)


def partner(head, turn):
    far, near = turn % 4, turn // 4
    mask = (far // 2 * 2 + (far % 2 + far // 2) % 2) * (HEADS // 4) + near
    return sum(flip(head, mask, bit) for bit in (1, 2, 4, 8))


def enter(head, member, team, hd_size):
    barrier = pltpu.get_barrier_semaphore()

    def greet(number):
        pl.semaphore_signal(barrier, inc=1, device_id=target(number, hd_size), device_id_type=MESH)

    @pl.loop(1, HEADS)
    def _(step):
        greet((head + step) % HEADS * team + member)

    @pl.loop(1, team)
    def _(step):
        greet(head * team + (member + step) % team)

    pl.semaphore_wait(barrier, HEADS - 1 + team - 1)


def columns(head):
    return pl.ds(pl.multiple_of(head * HEAD_DIM, HEAD_DIM), HEAD_DIM)


def dot(a, b, a_dim, b_dim):
    return lax.dot_general(
        a, b, (((a_dim,), (b_dim,)), ((), ())), preferred_element_type=jnp.float32
    )


def kernel(
    team, hd_size, pattern, q_in, k_in, v_in, g_in, o_out, dq_out, dk_out, dv_out,
    q_buf, g_buf, k_buf, v_buf, o_buf, dq_buf, window, chain, shared_sum, stage, theirs, summed,
    previous, latest, in_send, in_recv, in_own, pass_send, pass_recv,
    out_send, out_recv, out_own, team_send, team_recv,
):
    head, member = place(team, hd_size)
    blocks = k_buf.shape[0]
    scale = 1.0 / math.sqrt(HEAD_DIM)
    ins = (
        (k_in, lambda at: k_buf.at[at * team + member]),
        (v_in, lambda at: v_buf.at[at * team + member]),
        (q_in, lambda at: q_buf.at[at]),
        (g_in, lambda at: g_buf.at[at]),
    )
    outs = (
        (lambda at: o_buf.at[at], o_out),
        (lambda at: dq_buf.at[at], dq_out),
        (lambda at: summed.at[0, at], dk_out),
        (lambda at: summed.at[1, at], dv_out),
    )

    def receiver(turn):
        return partner(head, turn)

    sender = receiver

    def in_copy(number, peer, lands):
        source, dest = ins[number]
        return pltpu.make_async_remote_copy(
            source.at[:, columns(peer)], dest(lands), in_send.at[number, peer],
            in_recv.at[number, lands], device_id=target(peer * team + member, hd_size),
            device_id_type=MESH,
        )

    def in_local(number):
        source, dest = ins[number]
        return pltpu.make_async_copy(source.at[:, columns(head)], dest(head), in_own.at[number])

    def pass_copy(number, at, other, owner):
        ref = (k_buf, v_buf)[number].at[at * team + owner]
        return pltpu.make_async_remote_copy(
            ref, ref, pass_send.at[number, at, other], pass_recv.at[number, at, owner],
            device_id=target(head * team + other, hd_size), device_id_type=MESH,
        )

    def out_copy(number, peer, lands):
        source, dest = outs[number]
        return pltpu.make_async_remote_copy(
            source(peer), dest.at[:, columns(lands)], out_send.at[number, peer],
            out_recv.at[number, lands], device_id=target(peer * team + member, hd_size),
            device_id_type=MESH,
        )

    def out_local(number):
        source, dest = outs[number]
        return pltpu.make_async_copy(source(head), dest.at[:, columns(head)], out_own.at[number])

    def team_copy(number, at, step):
        return pltpu.make_async_remote_copy(
            stage.at[step - 1, number, at], theirs.at[step - 1, number, at],
            team_send.at[step - 1, number, at], team_recv.at[step - 1, number, at],
            device_id=target(head * team + (member + step) % team, hd_size), device_id_type=MESH,
        )

    def share(number, at):
        @pl.loop(1, team)
        def _(step):
            pass_copy(number, at, (member + step) % team, member).start()

    for number in range(4):
        in_local(number).start()
    enter(head, member, team, hd_size)

    for pair in ((0, 1), (2, 3)):
        @pl.loop(1, HEADS)
        def _(turn):
            peer = receiver(turn)
            for number in pair:
                in_copy(number, peer, head).start()

    for number in range(4):
        in_local(number).wait()
    for number in range(2):
        share(number, head)

    names = [
        pattern[r, sender(turn) * team + member] for turn in range(HEADS) for r in range(RANDOM)
    ]
    for later in range(len(names)):
        found = jnp.int32(-1)
        for earlier in range(later):
            found = jnp.where(names[earlier] == names[later], earlier, found)
        previous[later] = found

    @pl.loop(0, blocks)
    def _(block):
        found = jnp.int32(-1)
        for entry, name in enumerate(names):
            found = jnp.where(name == block, entry, found)
        latest[block] = found

    zeros = jnp.zeros((BLOCK, HEAD_DIM), jnp.float32)
    for number in range(2):
        shared_sum[number] = zeros
        for role in (0, 2):
            for at in (0, HEADS + 1):
                window[number, role, at] = zeros.astype(window.dtype)

    @pl.loop(1, HEADS)
    def _(turn):
        peer = sender(turn)
        for number in range(2):
            in_copy(number, head, peer).wait_recv()
            share(number, peer)

    @pl.loop(1, team)
    def _(step):
        other = (member + step) % team

        @pl.loop(0, HEADS)
        def _(turn):
            at = sender(turn)
            for number in range(2):
                pass_copy(number, at, other, other).wait_recv()

    def attend(turn, at):
        block = at * team + member
        ids = [jnp.maximum(block - 1, 0), block, jnp.minimum(block + 1, blocks - 1)]
        ids += list(range(GLOBALS)) + [pattern[r, block] for r in range(RANDOM)]
        allowed = [block >= 1, None, block + 1 < blocks] + [None] * (GLOBALS + RANDOM)
        queries, cotangent = q_buf[at], g_buf[at]
        keys = jnp.concatenate([k_buf[i] for i in ids], axis=0)
        values = jnp.concatenate([v_buf[i] for i in ids], axis=0)
        scores = dot(keys, queries, 1, 1) * scale
        parts = []
        for entry, ok in enumerate(allowed):
            part = scores[entry * BLOCK : (entry + 1) * BLOCK]
            parts.append(part if ok is None else jnp.where(ok, part, MASK_VALUE))
        scores = jnp.concatenate(parts, axis=0)
        weights = jnp.exp(scores - jnp.max(scores, axis=0, keepdims=True))
        total = jnp.sum(weights, axis=0, keepdims=True)
        soft = (weights * (1.0 / total)).astype(jnp.bfloat16)
        prob_grad = dot(values, cotangent, 1, 1)
        wide = soft.astype(jnp.float32)
        delta = jnp.sum(wide * prob_grad, axis=0, keepdims=True)
        score_grad = (wide * ((prob_grad - delta) * scale)).astype(jnp.bfloat16)
        o_buf[at] = dot(soft, values, 0, 0).astype(o_buf.dtype)
        dq_buf[at] = dot(score_grad, keys, 0, 0).astype(dq_buf.dtype)
        terms = (dot(score_grad, queries, 1, 0), dot(soft, cotangent, 1, 0))
        for number, term in enumerate(terms):
            entries = [term[e * BLOCK : (e + 1) * BLOCK] for e in range(len(ids))]
            for role in range(3):
                window[number, role, at + 1] = entries[role].astype(window.dtype)
            shared_sum[number] += entries[3]
            for r in range(RANDOM):
                slot = turn * RANDOM + r
                before = previous[slot]
                held = chain[number, jnp.maximum(before, 0)]
                chain[number, slot] = entries[3 + GLOBALS + r] + jnp.where(before >= 0, held, 0.0)

    @pl.loop(0, HEADS)
    def _(turn):
        at = sender(turn)

        @pl.when(turn > 0)
        def _():
            for number in (2, 3):
                in_copy(number, head, at).wait_recv()

        attend(turn, at)

        @pl.when(turn > 1)
        def _():
            before = sender(turn - 1)
            for number in range(2):
                out_copy(number, before, head).start()

    def base(number, block):
        last = latest[block]
        total = jnp.where(last >= 0, chain[number, jnp.maximum(last, 0)], 0.0)
        return total + jnp.where(block == 0, shared_sum[number], 0.0)

    def prepare(at, step):
        block = at * team + (member + step) % team
        for number in range(2):
            total = base(number, block)
            right = window[number, 2, at + 1 - (member + 1) // team].astype(jnp.float32)
            left = window[number, 0, at + 1 + (team - member) // team].astype(jnp.float32)
            total += jnp.where(step == 1, right, 0.0) + jnp.where(step == team - 1, left, 0.0)
            stage[step - 1, number, at] = total.astype(stage.dtype)

    last_peer = sender(HEADS - 1)
    for number in range(2):
        out_copy(number, last_peer, head).start()
        out_local(number).start()

    @pl.loop(1, HEADS + 2)
    def _(turn):
        @pl.when(turn <= HEADS)
        def _():
            @pl.loop(1, team)
            def _(step):
                prepare(receiver(turn % HEADS), step)

        @pl.when(turn > 1)
        def _():
            @pl.loop(1, team)
            def _(step):
                for number in range(2):
                    team_copy(number, receiver((turn - 1) % HEADS), step).start()

    @pl.loop(1, HEADS + 1)
    def _(turn):
        at = receiver(turn % HEADS)

        @pl.loop(1, team)
        def _(step):
            for number in range(2):
                team_copy(number, at, step).wait_recv()

        for number in range(2):
            own = base(number, at * team + member)
            own += window[number, 1, at + 1].astype(jnp.float32)
            summed[number, at] = lax.fori_loop(
                0, team - 1,
                lambda step, total: total + theirs[step, number, at].astype(jnp.float32), own,
            ).astype(summed.dtype)

        @pl.when(turn > 1)
        def _():
            for number in (2, 3):
                out_copy(number, receiver(turn - 1), head).start()

    for number in (2, 3):
        out_local(number).start()

    @pl.loop(1, HEADS)
    def _(turn):
        to, source = receiver(turn), sender(turn)
        for number in range(4):
            in_copy(number, to, head).wait_send()
            out_copy(number, to, head).wait_send()
            out_copy(number, head, source).wait_recv()

    @pl.loop(1, team)
    def _(step):
        @pl.loop(0, HEADS)
        def _(at):
            for number in range(2):
                pass_copy(number, at, (member + step) % team, member).wait_send()
                team_copy(number, at, step).wait_send()

    for number in range(4):
        out_local(number).wait()


def finish(*refs):
    ins, outs, held, loaded, stored = refs[:4], refs[4:8], refs[8], refs[9], refs[10]
    loads = [pltpu.make_async_copy(ins[i], held.at[i], loaded.at[i]) for i in range(4)]
    stores = [pltpu.make_async_copy(held.at[i], outs[i], stored.at[i]) for i in range(4)]
    for load in loads:
        load.start()
    for load, store in zip(loads, stores):
        load.wait()
        store.start()
    for store in stores:
        store.wait()


def on_device(query_states, key_states, value_states, output_cotangent, pattern):
    hd_size = lax.axis_size("hd")
    devices = lax.axis_size("grp") * hd_size
    team = devices // HEADS
    blocks = pattern.shape[0]
    bf16, f32 = jnp.bfloat16, jnp.float32
    dma = pltpu.SemaphoreType.DMA
    anywhere = pl.BlockSpec(memory_space=pl.ANY)
    tile = (BLOCK, HEAD_DIM)
    out_shape = jax.ShapeDtypeStruct(query_states.shape, bf16)
    results = pl.pallas_call(
        functools.partial(kernel, team, hd_size),
        out_shape=(out_shape,) * 4,
        in_specs=[pl.BlockSpec(memory_space=pltpu.SMEM)] + [anywhere] * 4,
        out_specs=(anywhere,) * 4,
        scratch_shapes=[
            pltpu.VMEM((HEADS, *tile), bf16),
            pltpu.VMEM((HEADS, *tile), bf16),
            pltpu.VMEM((blocks, *tile), bf16),
            pltpu.VMEM((blocks, *tile), bf16),
            pltpu.VMEM((HEADS, *tile), bf16),
            pltpu.VMEM((HEADS, *tile), bf16),
            pltpu.VMEM((2, 3, HEADS + 2, *tile), bf16),
            pltpu.VMEM((2, HEADS * RANDOM, *tile), f32),
            pltpu.VMEM((2, *tile), f32),
            pltpu.VMEM((team - 1, 2, HEADS, *tile), bf16),
            pltpu.VMEM((team - 1, 2, HEADS, *tile), bf16),
            pltpu.VMEM((2, HEADS, *tile), bf16),
            pltpu.SMEM((HEADS * RANDOM,), jnp.int32),
            pltpu.SMEM((blocks,), jnp.int32),
            dma((4, HEADS)), dma((4, HEADS)), dma((4,)),
            dma((2, HEADS, team)), dma((2, HEADS, team)),
            dma((4, HEADS)), dma((4, HEADS)), dma((4,)),
            dma((team - 1, 2, HEADS)), dma((team - 1, 2, HEADS)),
        ],
        compiler_params=pltpu.CompilerParams(
            collective_id=0, has_side_effects=True, vmem_limit_bytes=VMEM_BYTES
        ),
        name="head_attention",
    )(pattern.T, query_states, key_states, value_states, output_cotangent)
    return pl.pallas_call(
        finish,
        out_shape=(out_shape,) * 4,
        in_specs=[anywhere] * 4,
        out_specs=(anywhere,) * 4,
        scratch_shapes=[pltpu.VMEM((4, *query_states.shape), bf16), dma((4,)), dma((4,))],
        name="finish",
    )(*results)


def solution(mesh):
    split = P(("grp", "hd"), None)
    return jax.shard_map(
        on_device, mesh=mesh, in_specs=(split,) * 4 + (P(),), out_specs=(split,) * 4,
        check_vma=False,
    )
```
